32 devices in a mesh: groups: 1, cells: 32 (over z, y, x, core).
Axes of the slice: x: 2, y: 2, z: 4, core: 2. Of those that a mesh axis runs over, the one named last changes fastest.
Arguments:
- rna_counts: bfloat16 [2048, 4096], P(('groups', 'cells')), may hold values from 1 to 30, as said below
- atac_counts: bfloat16 [2048, 16384], P(('groups', 'cells')), may hold values from 1 to 30, as said below
- cell_factor: float32 [64, 2048], P(None, ('groups', 'cells')), may hold values from 0.1 to 3, as said below
- gene_factor: float32 [64, 4096], P(None, ('groups', 'cells')), may hold values from 0.1 to 3, as said below
- peak_factor: float32 [64, 16384], P(None, ('groups', 'cells')), may hold values from 0.1 to 3, as said below
- link_gene: int32 [256], P(('groups', 'cells')), may hold values from 0 to 31
- link_peak: int32 [256], P(('groups', 'cells')), may hold values from 0 to 127
- link_weight: int32 [256], P(('groups', 'cells')), may hold values from 1 to 4
- link_count: int32 [32], P(('groups', 'cells')), may hold values from 1 to 8, as said below
Outputs:
- cell_out: float32 [64, 2048], P(None, ('groups', 'cells'))
- gene_out: float32 [64, 4096], P(None, ('groups', 'cells'))
- peak_out: float32 [64, 16384], P(None, ('groups', 'cells'))
The draws below stay inside these ranges and needn't reach their ends.
Inputs may be any that keep to these rules, and one draw needn't show every extreme that they name: `rna_counts`: nonnegative counts. `atac_counts`: nonnegative counts. `cell_factor`: positive loadings. `gene_factor`: positive loadings. `peak_factor`: positive loadings. `link_count`: at least one live slot on every index, and some index has all 8 slots live.
All inputs are finite; a program needn't handle non-finite values.
Results may differ from the reference program's by a relative error of at most 0.00068.
Values may be sent and summed in bfloat16 or wider, within the bound.
A program may use at most 64 MiB of HBM per device.

```python
import jax
import jax.numpy as jnp
from jax import lax

K = 64
G = 4096
P_SIZE = 16384
BLOCK = 128
LINK_MAX = 8
ROUNDS = 2
CELLS = 2048
LINKS = 256
N_CELLS = 32


def draw_loadings(key, columns):
    base = jnp.exp(jax.random.uniform(key, (K, columns), jnp.float32, jnp.log(0.1), 0.0))
    rising = 1.0 + jnp.arange(columns, dtype=jnp.float32) / columns
    return base * rising[None, :]


def draw_counts(key, columns, salt):
    cell_key = jax.random.fold_in(key, 31)
    feature_key = jax.random.fold_in(key, salt)
    noise_key = jax.random.fold_in(key, salt + 1)
    cell_part = jnp.exp(1.5 * jax.random.normal(cell_key, (CELLS, K), jnp.float32))
    feature_part = jnp.exp(2.0 * jax.random.normal(feature_key, (K, columns), jnp.float32))
    noise = jnp.exp(0.4 * jax.random.normal(noise_key, (CELLS, columns), jnp.float32))
    planted = jnp.dot(cell_part, feature_part) / (3.0 * K)
    return jnp.clip(planted * noise, 1.0, 30.0).astype(jnp.bfloat16)


def draw_rna_counts(key, part):
    return draw_counts(key, G, 41)


def draw_atac_counts(key, part):
    return draw_counts(key, P_SIZE, 51)


def draw_cell_factor(key, part):
    return draw_loadings(jax.random.fold_in(key, 11), CELLS)


def draw_gene_factor(key, part):
    return draw_loadings(jax.random.fold_in(key, 12), G)


def draw_peak_factor(key, part):
    return draw_loadings(jax.random.fold_in(key, 13), P_SIZE)


def draw_link_count(key, part):
    counts = jax.random.randint(jax.random.fold_in(key, 21), (N_CELLS,), 1, LINK_MAX + 1)
    fullest = jax.random.randint(jax.random.fold_in(key, 22), (), 0, N_CELLS)
    return jnp.where(jnp.arange(N_CELLS, dtype=jnp.int32) == fullest, LINK_MAX, counts).astype(jnp.int32)


def plant(drawn, rng, low, top_value):
    index_at = [jax.random.randint(jax.random.fold_in(rng, axis), (), 0, length) for axis, length in enumerate(drawn.shape)]
    main_axis = drawn.shape.index(max(drawn.shape))
    beside = index_at[:main_axis] + [(index_at[main_axis] + 1) % drawn.shape[main_axis]] + index_at[main_axis + 1:]
    return drawn.at[tuple(index_at)].set(low).at[tuple(beside)].set(top_value)


def setup_inputs(seed: int = 0, part: int = 0) -> dict:
    arg_keys = jax.random.split(jax.random.key(seed), 10)
    part_keys = jax.random.split(jax.random.fold_in(arg_keys[9], part), 10)
    return {
        "rna_counts": draw_rna_counts(jax.random.fold_in(jax.random.fold_in(arg_keys[9], part), 71), part),
        "atac_counts": draw_atac_counts(jax.random.fold_in(jax.random.fold_in(arg_keys[9], part), 71), part),
        "cell_factor": draw_cell_factor(jax.random.fold_in(jax.random.fold_in(arg_keys[9], part), 71), part),
        "gene_factor": draw_gene_factor(jax.random.fold_in(jax.random.fold_in(arg_keys[9], part), 71), part),
        "peak_factor": draw_peak_factor(jax.random.fold_in(jax.random.fold_in(arg_keys[9], part), 71), part),
        "link_gene": plant(jax.random.randint(part_keys[5], (LINKS,), 0, G // BLOCK), jax.random.fold_in(part_keys[5], 1), 0, (G // BLOCK) - 1).astype(jnp.int32),
        "link_peak": plant(jax.random.randint(part_keys[6], (LINKS,), 0, P_SIZE // BLOCK), jax.random.fold_in(part_keys[6], 1), 0, (P_SIZE // BLOCK) - 1).astype(jnp.int32),
        "link_weight": plant(jax.random.randint(part_keys[7], (LINKS,), 1, 5), jax.random.fold_in(part_keys[7], 1), 1, 4).astype(jnp.int32),
        "link_count": draw_link_count(jax.random.fold_in(jax.random.fold_in(arg_keys[9], part), 71), part),
    }


EPSILON = 1e-6


def block_table(link_gene, link_peak, link_weight, link_count):
    live_slots = jnp.arange(LINK_MAX, dtype=jnp.int32)[None, :] < link_count[:, None]
    live_weight = jnp.where(live_slots.reshape(LINKS), link_weight, 0).astype(jnp.float32)
    gene_hot = (link_gene[:, None] == jnp.arange(G // BLOCK, dtype=jnp.int32)[None, :]).astype(jnp.float32)
    peak_hot = (link_peak[:, None] == jnp.arange(P_SIZE // BLOCK, dtype=jnp.int32)[None, :]).astype(jnp.float32)
    return jnp.dot((gene_hot * live_weight[:, None]).T, peak_hot, precision=lax.Precision.HIGHEST)


def couple(link_table, source):
    blocked = source.astype(jnp.float32).reshape(K, link_table.shape[1], BLOCK)
    result = jnp.einsum("kpc,gp->kgc", blocked, link_table, precision=lax.Precision.HIGHEST)
    return result.reshape(K, link_table.shape[0] * BLOCK)


def reference(rna_counts, atac_counts, cell_factor, gene_factor, peak_factor, link_gene, link_peak, link_weight, link_count):
    link_table = block_table(link_gene, link_peak, link_weight, link_count)
    link_scale = CELLS / 4.0
    for sweep_index in range(ROUNDS):
        cell_low = cell_factor.astype(jnp.bfloat16)
        gram_cells = jnp.dot(cell_factor, cell_factor.T, precision=lax.Precision.HIGHEST)
        gene_low = gene_factor.astype(jnp.bfloat16)
        peak_low = peak_factor.astype(jnp.bfloat16)
        gene_num = jnp.dot(cell_low, rna_counts, preferred_element_type=jnp.float32) + link_scale * couple(link_table, peak_low)
        peak_num = jnp.dot(cell_low, atac_counts, preferred_element_type=jnp.float32) + link_scale * couple(link_table.T, gene_low)
        gene_factor = gene_factor * gene_num / (jnp.dot(gram_cells, gene_factor, precision=lax.Precision.HIGHEST) + EPSILON)
        peak_factor = peak_factor * peak_num / (jnp.dot(gram_cells, peak_factor, precision=lax.Precision.HIGHEST) + EPSILON)
        gene_new = gene_factor.astype(jnp.bfloat16)
        peak_new = peak_factor.astype(jnp.bfloat16)
        gram_features = jnp.dot(gene_new, gene_new.T, preferred_element_type=jnp.float32) + jnp.dot(peak_new, peak_new.T, preferred_element_type=jnp.float32)
        cell_num = jnp.dot(gene_new, rna_counts.T, preferred_element_type=jnp.float32) + jnp.dot(peak_new, atac_counts.T, preferred_element_type=jnp.float32)
        cell_factor = cell_factor * cell_num / (jnp.dot(gram_features, cell_factor, precision=lax.Precision.HIGHEST) + EPSILON)
    return cell_factor, gene_factor, peak_factor
```

```python
import functools

import jax
import jax.numpy as jnp
from jax import lax
from jax.experimental import pallas as pl
from jax.experimental.pallas import tpu as pltpu
from jax.sharding import PartitionSpec as P

BLOCK = 128
ROUNDS = 2
EPSILON = 1e-06
HIGHEST = lax.Precision.HIGHEST
MESH = pl.DeviceIdType.MESH


def exchange_kernel(n, kinds, *refs):
    count = len(kinds)
    ins, outs = refs[:count], refs[count : 2 * count]
    send_sem, recv_sem, own_sem = refs[2 * count :]
    me = lax.axis_index("cells")

    def part(index, peer):
        kind = kinds[index]
        if kind == "all":
            return ins[index]
        if kind == "columns":
            width = outs[index].shape[2]
            return ins[index].at[:, pl.ds(pl.multiple_of(peer * width, 128), width)]
        return ins[index].at[peer]

    def remote(index, step, peer, slot):
        return pltpu.make_async_remote_copy(
            src_ref=part(index, peer),
            dst_ref=outs[index].at[slot],
            send_sem=send_sem.at[index, step],
            recv_sem=recv_sem.at[index, step],
            device_id={"cells": peer},
            device_id_type=MESH,
        )

    barrier = pltpu.get_barrier_semaphore()

    def greet(step, carry):
        pl.semaphore_signal(
            barrier, inc=1, device_id={"cells": lax.rem(me + step, n)}, device_id_type=MESH
        )
        return carry

    lax.fori_loop(1, n, greet, 0)
    own = [
        pltpu.make_async_copy(part(index, me), outs[index].at[me], own_sem.at[index])
        for index in range(count)
    ]
    for copy in own:
        copy.start()
    pl.semaphore_wait(barrier, n - 1)

    def send(step, carry):
        peer = lax.rem(me + step, n)
        for index in range(count):
            remote(index, step, peer, me).start()
        return carry

    lax.fori_loop(1, n, send, 0)

    def finish(step, carry):
        source = lax.rem(me + n - step, n)
        peer = lax.rem(me + step, n)
        for index in range(count):
            remote(index, step, peer, source).wait_recv()
            remote(index, step, peer, me).wait_send()
        return carry

    lax.fori_loop(1, n, finish, 0)
    for copy in own:
        copy.wait()


def exchange(n, collective_id, items):
    kinds = tuple(kind for kind, _ in items)
    shapes = []
    for kind, array in items:
        if kind == "all":
            shape = (n,) + array.shape
        elif kind == "columns":
            shape = (n, array.shape[0], array.shape[1] // n)
        else:
            shape = array.shape
        shapes.append(jax.ShapeDtypeStruct(shape, array.dtype))
    count = len(items)
    return pl.pallas_call(
        functools.partial(exchange_kernel, n, kinds),
        out_shape=tuple(shapes),
        in_specs=[pl.BlockSpec(memory_space=pl.ANY)] * count,
        out_specs=tuple([pl.BlockSpec(memory_space=pl.ANY)] * count),
        scratch_shapes=[
            pltpu.SemaphoreType.DMA((count, n)),
            pltpu.SemaphoreType.DMA((count, n)),
            pltpu.SemaphoreType.DMA((count,)),
        ],
        compiler_params=pltpu.CompilerParams(collective_id=collective_id, has_side_effects=True),
        name=f"exchange_{collective_id}",
    )(*[array for _, array in items])


def fold(array):
    half = array.shape[0] // 2
    return jnp.concatenate([array[:half], array[half:]], axis=1)


def unfold(array):
    half = array.shape[1] // 2
    return jnp.concatenate([array[:, :half], array[:, half:]], axis=0)


def fold_parts(array, n):
    rank, columns = array.shape
    width = columns // n
    return (
        array.reshape(2, rank // 2, n, width).transpose(2, 1, 0, 3).reshape(n, rank // 2, 2 * width)
    )


def unfold_whole(parts):
    n, half, width = parts.shape
    return (
        parts.reshape(n, half, 2, width // 2).transpose(2, 1, 0, 3).reshape(2 * half, n * width // 2)
    )


def counts_item(counts, n):
    rows, columns = counts.shape
    width = columns // n
    if width % 128 == 0:
        return ("columns", counts)
    return ("parts", counts.reshape(rows, n, width).transpose(1, 0, 2))


def column_parts(array, n):
    rank, columns = array.shape
    return array.reshape(rank, n, columns // n).transpose(1, 0, 2)


def pack_links(link_gene, link_peak, link_weight, link_count):
    slots = link_gene.shape[0]
    live = jnp.where(jnp.arange(slots, dtype=jnp.int32) < link_count[0], link_weight, 0)
    rows = jnp.stack([link_gene, link_peak, live])
    return jnp.zeros((8, 128), jnp.int32).at[:3, :slots].set(rows)


def table_of(packed, slots, gene_blocks, peak_blocks):
    gene, peak, live = [packed[:, row, :slots].reshape(-1) for row in range(3)]
    gene_hot = (gene[None, :] == jnp.arange(gene_blocks, dtype=jnp.int32)[:, None]).astype(
        jnp.float32
    ) * live.astype(jnp.float32)[None, :]
    peak_hot = (peak[:, None] == jnp.arange(peak_blocks, dtype=jnp.int32)[None, :]).astype(
        jnp.float32
    )
    return jnp.dot(gene_hot, peak_hot, precision=HIGHEST)


def own_rows(table, columns, me):
    rows = max(columns // BLOCK, 1)
    return lax.dynamic_slice_in_dim(table, me * columns // BLOCK, rows, axis=0)


def couple_all(own_table, source):
    blocked = source.astype(jnp.float32).reshape(source.shape[0], own_table.shape[1], BLOCK)
    mixed = jnp.einsum("kpc,gp->kgc", blocked, own_table, precision=HIGHEST)
    return mixed.reshape(source.shape[0], own_table.shape[0] * BLOCK)


def couple_own(own_table, whole, columns, me):
    rank = whole.shape[0]
    blocked = whole.astype(jnp.float32).reshape(rank, own_table.shape[1], BLOCK)
    if columns < BLOCK:
        blocked = lax.dynamic_slice_in_dim(blocked, lax.rem(me * columns, BLOCK), columns, axis=2)
    mixed = jnp.einsum("kpc,gp->kgc", blocked, own_table, precision=HIGHEST)
    return mixed.reshape(rank, columns)


def shards(
    rna_counts,
    atac_counts,
    cell_factor,
    gene_factor,
    peak_factor,
    link_gene,
    link_peak,
    link_weight,
    link_count,
):
    n = lax.axis_size("cells")
    me = lax.axis_index("cells")
    cells = rna_counts.shape[0]
    gene_width, peak_width = gene_factor.shape[1], peak_factor.shape[1]
    gene_blocks, peak_blocks = n * gene_width // BLOCK, n * peak_width // BLOCK
    link_scale = cells * n / 4.0

    (packed,) = exchange(
        n, 0, [("all", pack_links(link_gene, link_peak, link_weight, link_count))]
    )
    table = table_of(packed, link_gene.shape[0], gene_blocks, peak_blocks)
    to_peaks = own_rows(table.T, peak_width, me)

    def gene_share(peak_state):
        return column_parts(couple_all(to_peaks.T, peak_state.astype(jnp.bfloat16)), n)

    rna_all, atac_all, cell_parts, gene_parts, share_parts = exchange(
        n,
        1,
        [
            counts_item(rna_counts, n),
            counts_item(atac_counts, n),
            ("all", fold(cell_factor)),
            ("all", gene_factor.astype(jnp.bfloat16)),
            ("parts", gene_share(peak_factor)),
        ],
    )
    rna_all = rna_all.reshape(n * cells, gene_width)
    atac_all = atac_all.reshape(n * cells, peak_width)
    gene_state, peak_state = gene_factor, peak_factor
    for sweep_index in range(ROUNDS):
        cell_whole = unfold_whole(cell_parts)
        gram_cells = jnp.dot(cell_whole, cell_whole.T, precision=HIGHEST)
        cell_low = cell_whole.astype(jnp.bfloat16)
        gene_whole = gene_parts.transpose(1, 0, 2).reshape(gene_factor.shape[0], n * gene_width)
        gene_num = jnp.dot(
            cell_low, rna_all, preferred_element_type=jnp.float32
        ) + link_scale * jnp.sum(share_parts, axis=0)
        peak_num = jnp.dot(
            cell_low, atac_all, preferred_element_type=jnp.float32
        ) + link_scale * couple_own(to_peaks, gene_whole, peak_width, me)
        gene_state = (
            gene_state * gene_num / (jnp.dot(gram_cells, gene_state, precision=HIGHEST) + EPSILON)
        )
        peak_state = (
            peak_state * peak_num / (jnp.dot(gram_cells, peak_state, precision=HIGHEST) + EPSILON)
        )
        gene_low = gene_state.astype(jnp.bfloat16)
        peak_low = peak_state.astype(jnp.bfloat16)
        gram_part = jnp.dot(gene_low, gene_low.T, preferred_element_type=jnp.float32) + jnp.dot(
            peak_low, peak_low.T, preferred_element_type=jnp.float32
        )
        contract = functools.partial(
            lax.dot_general,
            dimension_numbers=(((1,), (1,)), ((), ())),
            preferred_element_type=jnp.float32,
        )
        cell_part = contract(gene_low, rna_all) + contract(peak_low, atac_all)
        items = [("parts", fold_parts(cell_part, n)), ("all", fold(gram_part))]
        if sweep_index + 1 < ROUNDS:
            items += [("all", gene_low), ("parts", gene_share(peak_state))]
        num_parts, gram_parts, *rest = exchange(n, 2 + 2 * sweep_index, items)
        cell_num = unfold(jnp.sum(num_parts, axis=0))
        gram_features = unfold(jnp.sum(gram_parts, axis=0))
        cell_factor = (
            cell_factor
            * cell_num
            / (jnp.dot(gram_features, cell_factor, precision=HIGHEST) + EPSILON)
        )
        if sweep_index + 1 < ROUNDS:
            gene_parts, share_parts = rest
            (cell_parts,) = exchange(n, 3 + 2 * sweep_index, [("all", fold(cell_factor))])
    return (cell_factor, gene_state, peak_state)


def solution(mesh):
    rows = P(("groups", "cells"), None)
    columns = P(None, ("groups", "cells"))
    slots = P(("groups", "cells"))
    return jax.shard_map(
        shards,
        mesh=mesh,
        in_specs=(rows, rows, columns, columns, columns, slots, slots, slots, slots),
        out_specs=(columns, columns, columns),
        check_vma=False,
    )
```

```python
import functools

import jax
import jax.numpy as jnp
from jax import lax
from jax.experimental import pallas as pl
from jax.experimental.pallas import tpu as pltpu
from jax.sharding import PartitionSpec as P

BLOCK = 128
CORES = 2
ROW = 4
ROUNDS = 2
EPSILON = 1e-06
HIGHEST = lax.Precision.HIGHEST
MESH = pl.DeviceIdType.MESH


def exchange_kernel(n, kinds, *refs):
    count = len(kinds)
    ins, outs = refs[:count], refs[count : 2 * count]
    send_sem, recv_sem, own_sem = refs[2 * count :]
    me = lax.axis_index("cells")
    whole = [index for index in range(count) if kinds[index] == "all"]
    direct = [index for index in range(count) if kinds[index] != "all"]
    planes = n // (ROW * CORES)
    plane, row, core = me // (ROW * CORES), lax.rem(me // CORES, ROW), lax.rem(me, CORES)

    def place(plane_at, row_at, core_at):
        return (plane_at * ROW + row_at) * CORES + core_at

    def part(index, peer):
        kind = kinds[index]
        if kind == "all":
            return ins[index]
        if kind == "columns":
            width = outs[index].shape[2]
            return ins[index].at[:, pl.ds(pl.multiple_of(peer * width, 128), width)]
        return ins[index].at[peer]

    def remote(index, step, peer, slot, source=None):
        return pltpu.make_async_remote_copy(
            src_ref=part(index, peer) if source is None else source,
            dst_ref=outs[index].at[slot],
            send_sem=send_sem.at[index, step],
            recv_sem=recv_sem.at[index, step],
            device_id={"cells": peer},
            device_id_type=MESH,
        )

    def first(index, step):
        return remote(index, step, place(lax.rem(plane + step, planes), row, core), me)

    def second(index, step, turn, slot, source):
        peer = place(plane, (row + turn) % ROW, core)
        return remote(index, planes + step * (ROW - 1) + turn - 1, peer, slot, source)

    def third(index, step, turn, slot, source):
        peer = place(plane, row, 1 - core)
        return remote(index, planes * ROW + step * ROW + turn, peer, slot, source)

    def slot_of(step, turn, core_at):
        return place(lax.rem(plane + planes - step, planes), (row + ROW - turn) % ROW, core_at)

    barrier = pltpu.get_barrier_semaphore()

    def greet(step, carry):
        pl.semaphore_signal(
            barrier, inc=1, device_id={"cells": lax.rem(me + step, n)}, device_id_type=MESH
        )
        return carry

    lax.fori_loop(1, n, greet, 0)
    own = [
        pltpu.make_async_copy(part(index, me), outs[index].at[me], own_sem.at[index])
        for index in range(count)
    ]
    for copy in own:
        copy.start()
    pl.semaphore_wait(barrier, n - 1)

    def start_first(step, carry):
        for index in whole:
            first(index, step).start()
        return carry

    def start_direct(step, carry):
        peer = lax.rem(me + step, n)
        for index in direct:
            remote(index, step, peer, me).start()
        return carry

    if whole:
        lax.fori_loop(1, planes, start_first, 0)
        for index in whole:
            for turn in range(1, ROW):
                second(index, 0, turn, me, ins[index]).start()
            third(index, 0, 0, me, ins[index]).start()
    if direct:
        lax.fori_loop(1, n, start_direct, 0)
    if whole:

        def pass_first(step, carry):
            slot = slot_of(step, 0, core)
            for index in whole:
                block = outs[index].at[slot]
                remote(index, step, place(plane, row, 1 - core), slot, block).wait_recv()
                for turn in range(1, ROW):
                    second(index, step, turn, slot, block).start()
                third(index, step, 0, slot, block).start()
            return carry

        def pass_second(step, carry):
            for turn in range(1, ROW):
                slot = slot_of(step, turn, core)
                for index in whole:
                    block = outs[index].at[slot]
                    second(index, step, turn, slot, block).wait_recv()
                    third(index, step, turn, slot, block).start()
            return carry

        def end_third(step, carry):
            for turn in range(ROW):
                slot = slot_of(step, turn, 1 - core)
                for index in whole:
                    block = outs[index].at[slot]
                    third(index, step, turn, slot, block).wait_recv()
            return carry

        def end_sends(step, carry):
            for index in whole:
                for turn in range(ROW):
                    if turn:
                        second(index, step, turn, me, ins[index]).wait_send()
                    third(index, step, turn, me, ins[index]).wait_send()
            return carry

        def end_first(step, carry):
            for index in whole:
                first(index, step).wait_send()
            return carry

        lax.fori_loop(1, planes, pass_first, 0)
        lax.fori_loop(0, planes, pass_second, 0)
        lax.fori_loop(0, planes, end_third, 0)
        lax.fori_loop(1, planes, end_first, 0)
        lax.fori_loop(0, planes, end_sends, 0)

    def end_direct(step, carry):
        source = lax.rem(me + n - step, n)
        peer = lax.rem(me + step, n)
        for index in direct:
            remote(index, step, peer, source).wait_recv()
            remote(index, step, peer, me).wait_send()
        return carry

    if direct:
        lax.fori_loop(1, n, end_direct, 0)
    for copy in own:
        copy.wait()


def exchange(n, collective_id, items):
    kinds = tuple(kind for kind, _ in items)
    shapes = []
    for kind, array in items:
        if kind == "all":
            shape = (n,) + array.shape
        elif kind == "columns":
            shape = (n, array.shape[0], array.shape[1] // n)
        else:
            shape = array.shape
        shapes.append(jax.ShapeDtypeStruct(shape, array.dtype))
    count = len(items)
    return pl.pallas_call(
        functools.partial(exchange_kernel, n, kinds),
        out_shape=tuple(shapes),
        in_specs=[pl.BlockSpec(memory_space=pl.ANY)] * count,
        out_specs=tuple([pl.BlockSpec(memory_space=pl.ANY)] * count),
        scratch_shapes=[
            pltpu.SemaphoreType.DMA((count, n)),
            pltpu.SemaphoreType.DMA((count, n)),
            pltpu.SemaphoreType.DMA((count,)),
        ],
        compiler_params=pltpu.CompilerParams(collective_id=collective_id, has_side_effects=True),
        name=f"exchange_{collective_id}",
    )(*[array for _, array in items])


def fold(array):
    half = array.shape[-2] // 2
    return jnp.concatenate([array[..., :half, :], array[..., half:, :]], axis=-1)


def unfold(array):
    half = array.shape[-1] // 2
    return jnp.concatenate([array[..., :half], array[..., half:]], axis=-2)


def counts_item(counts, n):
    rows, columns = counts.shape
    width = columns // n
    if width % 128 == 0:
        return ("columns", counts)
    return ("parts", counts.reshape(rows, n, width).transpose(1, 0, 2))


def pack_links(link_gene, link_peak, link_weight, link_count):
    slots = link_gene.shape[0]
    live = jnp.where(jnp.arange(slots, dtype=jnp.int32) < link_count[0], link_weight, 0)
    rows = jnp.stack([link_gene, link_peak, live])
    return jnp.zeros((8, 128), jnp.int32).at[:3, :slots].set(rows)


def table_of(packed, slots, gene_blocks, peak_blocks):
    gene, peak, live = [packed[:, row, :slots].reshape(-1) for row in range(3)]
    gene_hot = (gene[None, :] == jnp.arange(gene_blocks, dtype=jnp.int32)[:, None]).astype(
        jnp.float32
    ) * live.astype(jnp.float32)[None, :]
    peak_hot = (peak[:, None] == jnp.arange(peak_blocks, dtype=jnp.int32)[None, :]).astype(
        jnp.float32
    )
    return jnp.dot(gene_hot, peak_hot, precision=HIGHEST)


def own_rows(table, columns, me):
    rows = max(columns // BLOCK, 1)
    return lax.dynamic_slice_in_dim(table, me * columns // BLOCK, rows, axis=0)


def couple(own_table, parts, columns, me):
    n, rank, width = parts.shape
    parts = parts.astype(jnp.float32)
    if width >= BLOCK:
        per = width // BLOCK
        table = own_table.reshape(own_table.shape[0], n, per)
        mixed = [
            sum(
                jnp.sum(
                    parts[:, :, j * BLOCK : (j + 1) * BLOCK] * table[r, :, j][:, None, None], axis=0
                )
                for j in range(per)
            )
            for r in range(own_table.shape[0])
        ]
    else:
        per = BLOCK // width
        split = parts.reshape(n // per, per, rank, width)
        mixed = []
        for r in range(own_table.shape[0]):
            pieces = jnp.sum(split * own_table[r][:, None, None, None], axis=0)
            mixed.append(jnp.concatenate([pieces[j] for j in range(per)], axis=1))
    mixed = mixed[0] if len(mixed) == 1 else jnp.concatenate(mixed, axis=1)
    if columns < BLOCK:
        mixed = lax.dynamic_slice_in_dim(mixed, lax.rem(me * columns, BLOCK), columns, axis=1)
    return mixed


def contract(left, right, axis_left, axis_right, **options):
    return lax.dot_general(
        left,
        right,
        (((axis_left,), (axis_right,)), ((), ())),
        preferred_element_type=jnp.float32,
        **options,
    )


def shards(
    rna_counts,
    atac_counts,
    cell_factor,
    gene_factor,
    peak_factor,
    link_gene,
    link_peak,
    link_weight,
    link_count,
):
    n = lax.axis_size("cells")
    me = lax.axis_index("cells")
    cells = rna_counts.shape[0]
    rank = cell_factor.shape[0]
    gene_width, peak_width = gene_factor.shape[1], peak_factor.shape[1]
    gene_blocks, peak_blocks = n * gene_width // BLOCK, n * peak_width // BLOCK
    link_scale = cells * n / 4.0

    packed, cell_parts, gene_parts, peak_parts, rna_all, atac_all = exchange(
        n,
        0,
        [
            ("all", pack_links(link_gene, link_peak, link_weight, link_count)),
            ("all", fold(cell_factor.T)),
            ("all", gene_factor.astype(jnp.bfloat16)),
            ("all", peak_factor.astype(jnp.bfloat16)),
            counts_item(rna_counts, n),
            counts_item(atac_counts, n),
        ],
    )
    table = table_of(packed, link_gene.shape[0], gene_blocks, peak_blocks)
    to_genes = own_rows(table, gene_width, me)
    to_peaks = own_rows(table.T, peak_width, me)
    rna_all = rna_all.reshape(n * cells, gene_width)
    atac_all = atac_all.reshape(n * cells, peak_width)
    gene_state, peak_state = gene_factor, peak_factor
    for sweep_index in range(ROUNDS):
        cell_whole = unfold(cell_parts).reshape(n * cells, rank)
        gram_cells = contract(cell_whole, cell_whole, 0, 0, precision=HIGHEST)
        cell_low = cell_whole.astype(jnp.bfloat16)
        gene_num = contract(cell_low, rna_all, 0, 0) + link_scale * couple(
            to_genes, peak_parts, gene_width, me
        )
        peak_num = contract(cell_low, atac_all, 0, 0) + link_scale * couple(
            to_peaks, gene_parts, peak_width, me
        )
        gene_state = (
            gene_state * gene_num / (jnp.dot(gram_cells, gene_state, precision=HIGHEST) + EPSILON)
        )
        peak_state = (
            peak_state * peak_num / (jnp.dot(gram_cells, peak_state, precision=HIGHEST) + EPSILON)
        )
        gene_low = gene_state.astype(jnp.bfloat16)
        peak_low = peak_state.astype(jnp.bfloat16)
        gram_part = contract(gene_low, gene_low, 1, 1) + contract(peak_low, peak_low, 1, 1)
        cell_part = contract(rna_all, gene_low, 1, 1) + contract(atac_all, peak_low, 1, 1)
        items = [
            ("all", fold(gram_part)),
            ("parts", fold(cell_part.reshape(n, cells, rank))),
        ]
        if sweep_index + 1 < ROUNDS:
            items += [("all", gene_low), ("all", peak_low)]
        gram_parts, num_parts, *rest = exchange(n, 1 + 2 * sweep_index, items)
        cell_num = unfold(jnp.sum(num_parts, axis=0)).T
        gram_features = unfold(jnp.sum(gram_parts, axis=0))
        cell_factor = (
            cell_factor
            * cell_num
            / (jnp.dot(gram_features, cell_factor, precision=HIGHEST) + EPSILON)
        )
        if sweep_index + 1 < ROUNDS:
            gene_parts, peak_parts = rest
            (cell_parts,) = exchange(n, 2 + 2 * sweep_index, [("all", fold(cell_factor.T))])
    return (cell_factor, gene_state, peak_state)


def solution(mesh):
    rows = P(("groups", "cells"), None)
    columns = P(None, ("groups", "cells"))
    slots = P(("groups", "cells"))
    return jax.shard_map(
        shards,
        mesh=mesh,
        in_specs=(rows, rows, columns, columns, columns, slots, slots, slots, slots),
        out_specs=(columns, columns, columns),
        check_vma=False,
    )
```

```python
import functools

import jax
import jax.numpy as jnp
from jax import lax
from jax.experimental import pallas as pl
from jax.experimental.pallas import tpu as pltpu
from jax.sharding import PartitionSpec as P

BLOCK = 128
CORES = 2
ROW = 4
ROUNDS = 2
EPSILON = 1e-06
HIGHEST = lax.Precision.HIGHEST
MESH = pl.DeviceIdType.MESH


class Routes:
    def __init__(self, n, kinds, ins, outs, send_sem, recv_sem, own_sem):
        self.n, self.kinds, self.ins, self.outs = n, kinds, ins, outs
        self.send_sem, self.recv_sem, self.own_sem = send_sem, recv_sem, own_sem
        self.me = lax.axis_index("cells")
        self.planes = n // (ROW * CORES)
        self.plane = self.me // (ROW * CORES)
        self.row = lax.rem(self.me // CORES, ROW)
        self.core = lax.rem(self.me, CORES)

    def greet(self):
        barrier = pltpu.get_barrier_semaphore()

        def signal(step, carry):
            peer = lax.rem(self.me + step, self.n)
            pl.semaphore_signal(
                barrier, inc=1, device_id={"cells": peer}, device_id_type=MESH
            )
            return carry

        lax.fori_loop(1, self.n, signal, 0)
        return lambda: pl.semaphore_wait(barrier, self.n - 1)

    def part(self, index, peer):
        kind = self.kinds[index]
        if kind == "all":
            return self.ins[index]
        if kind == "columns":
            width = self.outs[index].shape[2]
            return self.ins[index].at[:, pl.ds(pl.multiple_of(peer * width, 128), width)]
        return self.ins[index].at[peer]

    def own(self, index):
        return pltpu.make_async_copy(
            self.part(index, self.me), self.outs[index].at[self.me], self.own_sem.at[index]
        )

    def remote(self, index, step, peer, slot, source=None):
        return pltpu.make_async_remote_copy(
            src_ref=self.part(index, peer) if source is None else source,
            dst_ref=self.outs[index].at[slot],
            send_sem=self.send_sem.at[index, step],
            recv_sem=self.recv_sem.at[index, step],
            device_id={"cells": peer},
            device_id_type=MESH,
        )

    def place(self, plane_at, row_at, core_at):
        return (plane_at * ROW + row_at) * CORES + core_at

    def first(self, index, step):
        peer = self.place(lax.rem(self.plane + step, self.planes), self.row, self.core)
        return self.remote(index, step, peer, self.me)

    def second(self, index, step, turn, slot, source):
        peer = self.place(self.plane, (self.row + turn) % ROW, self.core)
        return self.remote(index, self.planes + step * (ROW - 1) + turn - 1, peer, slot, source)

    def third(self, index, step, turn, slot, source):
        peer = self.place(self.plane, self.row, 1 - self.core)
        return self.remote(index, self.planes * ROW + step * ROW + turn, peer, slot, source)

    def slot_of(self, step, turn, core_at):
        plane_at = lax.rem(self.plane + self.planes - step, self.planes)
        return self.place(plane_at, (self.row + ROW - turn) % ROW, core_at)

    def loop(self, low, high, body):
        def step_of(step, carry):
            body(step)
            return carry

        lax.fori_loop(low, high, step_of, 0)

    def start_all(self, items):
        def body(step):
            for index in items:
                self.first(index, step).start()

        self.loop(1, self.planes, body)
        for index in items:
            for turn in range(1, ROW):
                self.second(index, 0, turn, self.me, self.ins[index]).start()
            self.third(index, 0, 0, self.me, self.ins[index]).start()

    def relay_first(self, items):
        def body(step):
            slot = self.slot_of(step, 0, self.core)
            for index in items:
                block = self.outs[index].at[slot]
                self.remote(
                    index, step, self.place(self.plane, self.row, 1 - self.core), slot, block
                ).wait_recv()
                for turn in range(1, ROW):
                    self.second(index, step, turn, slot, block).start()
                self.third(index, step, 0, slot, block).start()

        self.loop(1, self.planes, body)

    def relay_second(self, items):
        def body(step):
            for turn in range(1, ROW):
                slot = self.slot_of(step, turn, self.core)
                for index in items:
                    block = self.outs[index].at[slot]
                    self.second(index, step, turn, slot, block).wait_recv()
                    self.third(index, step, turn, slot, block).start()

        self.loop(0, self.planes, body)

    def receive_third(self, items):
        def body(step):
            for turn in range(ROW):
                slot = self.slot_of(step, turn, 1 - self.core)
                for index in items:
                    self.third(index, step, turn, slot, self.outs[index].at[slot]).wait_recv()

        self.loop(0, self.planes, body)

    def end_all(self, items):
        def first(step):
            for index in items:
                self.first(index, step).wait_send()

        def later(step):
            for index in items:
                for turn in range(ROW):
                    if turn:
                        self.second(index, step, turn, self.me, self.ins[index]).wait_send()
                    self.third(index, step, turn, self.me, self.ins[index]).wait_send()

        self.loop(1, self.planes, first)
        self.loop(0, self.planes, later)

    def start_direct(self, items):
        def body(step):
            for index in items:
                self.remote(index, step, lax.rem(self.me + step, self.n), self.me).start()

        self.loop(1, self.n, body)

    def receive_direct(self, items):
        def body(step):
            source = lax.rem(self.me + self.n - step, self.n)
            peer = lax.rem(self.me + step, self.n)
            for index in items:
                self.remote(index, step, peer, source).wait_recv()

        self.loop(1, self.n, body)

    def end_direct(self, items):
        def body(step):
            for index in items:
                self.remote(index, step, lax.rem(self.me + step, self.n), self.me).wait_send()

        self.loop(1, self.n, body)


def exchange_kernel(n, kinds, *refs):
    count = len(kinds)
    routes = Routes(n, kinds, refs[:count], refs[count : 2 * count], *refs[2 * count :])
    whole = [index for index in range(count) if kinds[index] == "all"]
    direct = [index for index in range(count) if kinds[index] != "all"]
    greeted = routes.greet()
    for index in range(count):
        routes.own(index).start()
    greeted()
    routes.start_all(whole)
    if direct:
        routes.start_direct(direct)
    routes.relay_first(whole)
    routes.relay_second(whole)
    routes.receive_third(whole)
    if direct:
        routes.receive_direct(direct)
        routes.end_direct(direct)
    routes.end_all(whole)
    for index in range(count):
        routes.own(index).wait()


def between_kernel(
    n, gram, num, gene, peak, cell, gene_parts, peak_parts, cell_parts, cell_new,
    gram_parts, num_parts, *sems
):
    routes = Routes(
        n,
        ("all", "parts", "all", "all", "all"),
        (gram, num, gene, peak, cell_new),
        (gram_parts, num_parts, gene_parts, peak_parts, cell_parts),
        *sems,
    )
    greeted = routes.greet()
    for index in range(4):
        routes.own(index).start()
    greeted()
    routes.start_all([0])
    routes.start_direct([1])
    routes.start_all([2, 3])
    routes.relay_first([0])
    routes.relay_second([0])
    routes.relay_first([2, 3])
    routes.receive_third([0])
    routes.receive_direct([1])
    routes.own(0).wait()
    routes.own(1).wait()
    folded = jnp.sum(gram_parts[...], axis=0)
    rank = folded.shape[1] // 2
    turned = pltpu.roll(folded, rank, 1)
    left = lax.broadcasted_iota(jnp.int32, folded.shape, 1) < rank
    square = jnp.concatenate(
        [
            jnp.where(left, folded, 0.0),
            jnp.where(left, turned, 0.0),
            jnp.where(left, 0.0, turned),
            jnp.where(left, 0.0, folded),
        ],
        axis=0,
    )
    denominator = jnp.dot(
        cell[...], square, precision=HIGHEST, preferred_element_type=jnp.float32
    )
    cell_new[...] = cell[...] * jnp.sum(num_parts[...], axis=0) / (denominator + EPSILON)
    routes.own(4).start()
    routes.start_all([4])
    routes.relay_second([2, 3])
    routes.relay_first([4])
    routes.relay_second([4])
    routes.receive_third([2, 3, 4])
    routes.end_direct([1])
    routes.end_all([0, 2, 3, 4])
    for index in range(2, 5):
        routes.own(index).wait()


def between(n, collective_id, gram, num, gene, peak, cell):
    anywhere = pl.BlockSpec(memory_space=pl.ANY)
    vmem = pl.BlockSpec(memory_space=pltpu.VMEM)
    gathered = [jax.ShapeDtypeStruct((n,) + x.shape, x.dtype) for x in (gene, peak, cell)]
    return pl.pallas_call(
        functools.partial(between_kernel, n),
        out_shape=(*gathered, jax.ShapeDtypeStruct(cell.shape, cell.dtype)),
        in_specs=[anywhere] * 4 + [vmem],
        out_specs=(anywhere, anywhere, anywhere, vmem),
        scratch_shapes=[
            pltpu.VMEM((n,) + gram.shape, gram.dtype),
            pltpu.VMEM(num.shape, num.dtype),
            pltpu.SemaphoreType.DMA((5, n)),
            pltpu.SemaphoreType.DMA((5, n)),
            pltpu.SemaphoreType.DMA((5,)),
        ],
        compiler_params=pltpu.CompilerParams(collective_id=collective_id, has_side_effects=True),
        name=f"between_{collective_id}",
    )(gram, num, gene, peak, cell)


def exchange(n, collective_id, items):
    kinds = tuple(kind for kind, _ in items)
    shapes = []
    for kind, array in items:
        if kind == "all":
            shape = (n,) + array.shape
        elif kind == "columns":
            shape = (n, array.shape[0], array.shape[1] // n)
        else:
            shape = array.shape
        shapes.append(jax.ShapeDtypeStruct(shape, array.dtype))
    count = len(items)
    return pl.pallas_call(
        functools.partial(exchange_kernel, n, kinds),
        out_shape=tuple(shapes),
        in_specs=[pl.BlockSpec(memory_space=pl.ANY)] * count,
        out_specs=tuple([pl.BlockSpec(memory_space=pl.ANY)] * count),
        scratch_shapes=[
            pltpu.SemaphoreType.DMA((count, n)),
            pltpu.SemaphoreType.DMA((count, n)),
            pltpu.SemaphoreType.DMA((count,)),
        ],
        compiler_params=pltpu.CompilerParams(collective_id=collective_id, has_side_effects=True),
        name=f"exchange_{collective_id}",
    )(*[array for _, array in items])


def fold(array):
    half = array.shape[-2] // 2
    return jnp.concatenate([array[..., :half, :], array[..., half:, :]], axis=-1)


def unfold(array):
    half = array.shape[-1] // 2
    return jnp.concatenate([array[..., :half], array[..., half:]], axis=-2)


def counts_item(counts, n):
    rows, columns = counts.shape
    width = columns // n
    if width % 128 == 0:
        return ("columns", counts)
    return ("parts", counts.reshape(rows, n, width).transpose(1, 0, 2))


def pack_links(link_gene, link_peak, link_weight, link_count):
    slots = link_gene.shape[0]
    live = jnp.where(jnp.arange(slots, dtype=jnp.int32) < link_count[0], link_weight, 0)
    rows = jnp.stack([link_gene, link_peak, live])
    return jnp.zeros((8, 128), jnp.int32).at[:3, :slots].set(rows)


def table_of(packed, slots, gene_blocks, peak_blocks):
    gene, peak, live = [packed[:, row, :slots].reshape(-1) for row in range(3)]
    gene_hot = (gene[None, :] == jnp.arange(gene_blocks, dtype=jnp.int32)[:, None]).astype(
        jnp.float32
    ) * live.astype(jnp.float32)[None, :]
    peak_hot = (peak[:, None] == jnp.arange(peak_blocks, dtype=jnp.int32)[None, :]).astype(
        jnp.float32
    )
    return jnp.dot(gene_hot, peak_hot, precision=HIGHEST)


def own_rows(table, columns, me):
    rows = max(columns // BLOCK, 1)
    return lax.dynamic_slice_in_dim(table, me * columns // BLOCK, rows, axis=0)


def couple(own_table, parts, columns, me):
    n, rank, width = parts.shape
    parts = parts.astype(jnp.float32)
    if width >= BLOCK:
        per = width // BLOCK
        table = own_table.reshape(own_table.shape[0], n, per)
        mixed = [
            sum(
                jnp.sum(
                    parts[:, :, j * BLOCK : (j + 1) * BLOCK] * table[r, :, j][:, None, None], axis=0
                )
                for j in range(per)
            )
            for r in range(own_table.shape[0])
        ]
    else:
        per = BLOCK // width
        split = parts.reshape(n // per, per, rank, width)
        mixed = []
        for r in range(own_table.shape[0]):
            pieces = jnp.sum(split * own_table[r][:, None, None, None], axis=0)
            mixed.append(jnp.concatenate([pieces[j] for j in range(per)], axis=1))
    mixed = mixed[0] if len(mixed) == 1 else jnp.concatenate(mixed, axis=1)
    if columns < BLOCK:
        mixed = lax.dynamic_slice_in_dim(mixed, lax.rem(me * columns, BLOCK), columns, axis=1)
    return mixed


def contract(left, right, axis_left, axis_right, **options):
    return lax.dot_general(
        left,
        right,
        (((axis_left,), (axis_right,)), ((), ())),
        preferred_element_type=jnp.float32,
        **options,
    )


def shards(
    rna_counts,
    atac_counts,
    cell_factor,
    gene_factor,
    peak_factor,
    link_gene,
    link_peak,
    link_weight,
    link_count,
):
    n = lax.axis_size("cells")
    me = lax.axis_index("cells")
    cells = rna_counts.shape[0]
    rank = cell_factor.shape[0]
    gene_width, peak_width = gene_factor.shape[1], peak_factor.shape[1]
    gene_blocks, peak_blocks = n * gene_width // BLOCK, n * peak_width // BLOCK
    link_scale = cells * n / 4.0

    cell_state = fold(cell_factor.T)
    packed, cell_parts, gene_parts, peak_parts, rna_all, atac_all = exchange(
        n,
        0,
        [
            ("all", pack_links(link_gene, link_peak, link_weight, link_count)),
            ("all", cell_state),
            ("all", gene_factor.astype(jnp.bfloat16)),
            ("all", peak_factor.astype(jnp.bfloat16)),
            counts_item(rna_counts, n),
            counts_item(atac_counts, n),
        ],
    )
    table = table_of(packed, link_gene.shape[0], gene_blocks, peak_blocks)
    to_genes = own_rows(table, gene_width, me)
    to_peaks = own_rows(table.T, peak_width, me)
    rna_all = rna_all.reshape(n * cells, gene_width)
    atac_all = atac_all.reshape(n * cells, peak_width)
    gene_state, peak_state = gene_factor, peak_factor
    for sweep_index in range(ROUNDS):
        cell_whole = unfold(cell_parts).reshape(n * cells, rank)
        gram_cells = contract(cell_whole, cell_whole, 0, 0, precision=HIGHEST)
        cell_low = cell_whole.astype(jnp.bfloat16)
        gene_num = contract(cell_low, rna_all, 0, 0) + link_scale * couple(
            to_genes, peak_parts, gene_width, me
        )
        peak_num = contract(cell_low, atac_all, 0, 0) + link_scale * couple(
            to_peaks, gene_parts, peak_width, me
        )
        gene_state = (
            gene_state * gene_num / (jnp.dot(gram_cells, gene_state, precision=HIGHEST) + EPSILON)
        )
        peak_state = (
            peak_state * peak_num / (jnp.dot(gram_cells, peak_state, precision=HIGHEST) + EPSILON)
        )
        gene_low = gene_state.astype(jnp.bfloat16)
        peak_low = peak_state.astype(jnp.bfloat16)
        gram_part = contract(gene_low, gene_low, 1, 1) + contract(peak_low, peak_low, 1, 1)
        cell_part = contract(rna_all, gene_low, 1, 1) + contract(atac_all, peak_low, 1, 1)
        gram_item = fold(gram_part)
        num_item = fold(cell_part.reshape(n, cells, rank))
        if sweep_index + 1 < ROUNDS:
            gene_parts, peak_parts, cell_parts, cell_state = between(
                n, 1 + sweep_index, gram_item, num_item, gene_low, peak_low, cell_state
            )
    cell_factor = unfold(cell_state).T
    gram_parts, num_parts = exchange(n, ROUNDS, [("all", gram_item), ("parts", num_item)])
    cell_num = unfold(jnp.sum(num_parts, axis=0)).T
    gram_features = unfold(jnp.sum(gram_parts, axis=0))
    cell_factor = (
        cell_factor * cell_num / (jnp.dot(gram_features, cell_factor, precision=HIGHEST) + EPSILON)
    )
    return (cell_factor, gene_state, peak_state)


def solution(mesh):
    rows = P(("groups", "cells"), None)
    columns = P(None, ("groups", "cells"))
    slots = P(("groups", "cells"))
    return jax.shard_map(
        shards,
        mesh=mesh,
        in_specs=(rows, rows, columns, columns, columns, slots, slots, slots, slots),
        out_specs=(columns, columns, columns),
        check_vma=False,
    )
```

```python
import functools

import jax
import jax.numpy as jnp
from jax import lax
from jax.experimental import pallas as pl
from jax.experimental.pallas import tpu as pltpu
from jax.sharding import PartitionSpec as P

BLOCK = 128
CORES = 2
ROW = 4
ROUNDS = 2
EPSILON = 1e-06
HIGHEST = lax.Precision.HIGHEST
MESH = pl.DeviceIdType.MESH


class Routes:
    def __init__(self, n, kinds, ins, outs, send_sem, recv_sem, own_sem):
        self.n, self.kinds, self.ins, self.outs = n, kinds, ins, outs
        self.send_sem, self.recv_sem, self.own_sem = send_sem, recv_sem, own_sem
        self.me = lax.axis_index("cells")
        self.planes = n // (ROW * CORES)
        self.plane = self.me // (ROW * CORES)
        self.row = lax.rem(self.me // CORES, ROW)
        self.core = lax.rem(self.me, CORES)

    def greet(self):
        barrier = pltpu.get_barrier_semaphore()

        def signal(step, carry):
            peer = lax.rem(self.me + step, self.n)
            pl.semaphore_signal(
                barrier, inc=1, device_id={"cells": peer}, device_id_type=MESH
            )
            return carry

        lax.fori_loop(1, self.n, signal, 0)
        return lambda: pl.semaphore_wait(barrier, self.n - 1)

    def part(self, index, peer):
        kind = self.kinds[index]
        if kind == "all":
            return self.ins[index]
        if kind == "columns":
            width = self.outs[index].shape[2]
            return self.ins[index].at[:, pl.ds(pl.multiple_of(peer * width, 128), width)]
        return self.ins[index].at[peer]

    def own(self, index):
        return pltpu.make_async_copy(
            self.part(index, self.me), self.outs[index].at[self.me], self.own_sem.at[index]
        )

    def remote(self, index, step, peer, slot, source=None):
        return pltpu.make_async_remote_copy(
            src_ref=self.part(index, peer) if source is None else source,
            dst_ref=self.outs[index].at[slot],
            send_sem=self.send_sem.at[index, step],
            recv_sem=self.recv_sem.at[index, step],
            device_id={"cells": peer},
            device_id_type=MESH,
        )

    def place(self, plane_at, row_at, core_at):
        return (plane_at * ROW + row_at) * CORES + core_at

    def first(self, index, step):
        peer = self.place(lax.rem(self.plane + step, self.planes), self.row, self.core)
        return self.remote(index, step, peer, self.me)

    def second(self, index, step, turn, slot, source):
        peer = self.place(self.plane, (self.row + turn) % ROW, self.core)
        return self.remote(index, self.planes + step * (ROW - 1) + turn - 1, peer, slot, source)

    def third(self, index, step, turn, slot, source):
        peer = self.place(self.plane, self.row, 1 - self.core)
        return self.remote(index, self.planes * ROW + step * ROW + turn, peer, slot, source)

    def slot_of(self, step, turn, core_at):
        plane_at = lax.rem(self.plane + self.planes - step, self.planes)
        return self.place(plane_at, (self.row + ROW - turn) % ROW, core_at)

    def loop(self, low, high, body):
        def step_of(step, carry):
            body(step)
            return carry

        lax.fori_loop(low, high, step_of, 0)

    def start_all(self, items):
        def body(step):
            for index in items:
                self.first(index, step).start()

        self.loop(1, self.planes, body)
        for index in items:
            for turn in range(1, ROW):
                self.second(index, 0, turn, self.me, self.ins[index]).start()
            self.third(index, 0, 0, self.me, self.ins[index]).start()

    def relay_first(self, items):
        def body(step):
            slot = self.slot_of(step, 0, self.core)
            for index in items:
                block = self.outs[index].at[slot]
                self.remote(
                    index, step, self.place(self.plane, self.row, 1 - self.core), slot, block
                ).wait_recv()
                for turn in range(1, ROW):
                    self.second(index, step, turn, slot, block).start()
                self.third(index, step, 0, slot, block).start()

        self.loop(1, self.planes, body)

    def relay_second(self, items):
        def body(step):
            for turn in range(1, ROW):
                slot = self.slot_of(step, turn, self.core)
                for index in items:
                    block = self.outs[index].at[slot]
                    self.second(index, step, turn, slot, block).wait_recv()
                    self.third(index, step, turn, slot, block).start()

        self.loop(0, self.planes, body)

    def receive_third(self, items):
        def body(step):
            for turn in range(ROW):
                slot = self.slot_of(step, turn, 1 - self.core)
                for index in items:
                    self.third(index, step, turn, slot, self.outs[index].at[slot]).wait_recv()

        self.loop(0, self.planes, body)

    def end_all(self, items):
        def first(step):
            for index in items:
                self.first(index, step).wait_send()

        def later(step):
            for index in items:
                for turn in range(ROW):
                    if turn:
                        self.second(index, step, turn, self.me, self.ins[index]).wait_send()
                    self.third(index, step, turn, self.me, self.ins[index]).wait_send()

        self.loop(1, self.planes, first)
        self.loop(0, self.planes, later)

    def start_direct(self, items):
        def body(step):
            for index in items:
                self.remote(index, step, lax.rem(self.me + step, self.n), self.me).start()

        self.loop(1, self.n, body)

    def receive_direct(self, items):
        def body(step):
            source = lax.rem(self.me + self.n - step, self.n)
            peer = lax.rem(self.me + step, self.n)
            for index in items:
                self.remote(index, step, peer, source).wait_recv()

        self.loop(1, self.n, body)

    def end_direct(self, items):
        def body(step):
            for index in items:
                self.remote(index, step, lax.rem(self.me + step, self.n), self.me).wait_send()

        self.loop(1, self.n, body)


def exchange_kernel(n, kinds, *refs):
    count = len(kinds)
    ins, outs = list(refs[:count]), refs[count : 2 * count]
    casts = [index for index in range(count) if kinds[index] == "cast"]
    sems = refs[2 * count : 2 * count + 3]
    given = [ins[index] for index in casts]
    for index, low in zip(casts, refs[2 * count + 3 :]):
        ins[index] = low
    kinds = tuple("all" if kind == "cast" else kind for kind in kinds)
    routes = Routes(n, kinds, ins, outs, *sems)
    whole = [index for index in range(count) if kinds[index] == "all"]
    direct = [index for index in range(count) if kinds[index] != "all"]
    greeted = routes.greet()
    for index, wide in zip(casts, given):
        ins[index][...] = wide[...].astype(jnp.bfloat16)
    greeted()
    routes.start_all(whole)
    for index in range(count):
        routes.own(index).start()
    if direct:
        routes.start_direct(direct)
    routes.relay_first(whole)
    routes.relay_second(whole)
    routes.receive_third(whole)
    if direct:
        routes.receive_direct(direct)
        routes.end_direct(direct)
    routes.end_all(whole)
    for index in range(count):
        routes.own(index).wait()


def between_kernel(
    n, gram, num, gene, peak, cell, gene_parts, peak_parts, cell_parts, cell_new,
    gram_parts, num_parts, *sems
):
    routes = Routes(
        n,
        ("all", "parts", "all", "all", "all"),
        (gram, num, gene, peak, cell_new),
        (gram_parts, num_parts, gene_parts, peak_parts, cell_parts),
        *sems,
    )
    greeted = routes.greet()
    for index in range(4):
        routes.own(index).start()
    greeted()
    routes.start_all([0])
    routes.start_direct([1])
    routes.start_all([2, 3])
    routes.relay_first([0])
    routes.relay_second([0])
    routes.relay_first([2, 3])
    routes.receive_third([0])
    routes.receive_direct([1])
    routes.own(0).wait()
    routes.own(1).wait()
    folded = jnp.sum(gram_parts[...], axis=0)
    rank = folded.shape[1] // 2
    turned = pltpu.roll(folded, rank, 1)
    left = lax.broadcasted_iota(jnp.int32, folded.shape, 1) < rank
    square = jnp.concatenate(
        [
            jnp.where(left, folded, 0.0),
            jnp.where(left, turned, 0.0),
            jnp.where(left, 0.0, turned),
            jnp.where(left, 0.0, folded),
        ],
        axis=0,
    )
    denominator = jnp.dot(
        cell[...], square, precision=HIGHEST, preferred_element_type=jnp.float32
    )
    cell_new[...] = cell[...] * jnp.sum(num_parts[...], axis=0) / (denominator + EPSILON)
    routes.own(4).start()
    routes.start_all([4])
    routes.relay_second([2, 3])
    routes.relay_first([4])
    routes.relay_second([4])
    routes.receive_third([2, 3, 4])
    routes.end_direct([1])
    routes.end_all([0, 2, 3, 4])
    for index in range(2, 5):
        routes.own(index).wait()


def between(n, collective_id, gram, num, gene, peak, cell):
    anywhere = pl.BlockSpec(memory_space=pl.ANY)
    vmem = pl.BlockSpec(memory_space=pltpu.VMEM)
    gathered = [jax.ShapeDtypeStruct((n,) + x.shape, x.dtype) for x in (gene, peak, cell)]
    return pl.pallas_call(
        functools.partial(between_kernel, n),
        out_shape=(*gathered, jax.ShapeDtypeStruct(cell.shape, cell.dtype)),
        in_specs=[anywhere] * 4 + [vmem],
        out_specs=(anywhere, anywhere, anywhere, vmem),
        scratch_shapes=[
            pltpu.VMEM((n,) + gram.shape, gram.dtype),
            pltpu.VMEM(num.shape, num.dtype),
            pltpu.SemaphoreType.DMA((5, n)),
            pltpu.SemaphoreType.DMA((5, n)),
            pltpu.SemaphoreType.DMA((5,)),
        ],
        compiler_params=pltpu.CompilerParams(collective_id=collective_id, has_side_effects=True),
        name=f"between_{collective_id}",
    )(gram, num, gene, peak, cell)


def exchange(n, collective_id, items):
    kinds = tuple(kind for kind, _ in items)
    shapes = []
    for kind, array in items:
        if kind in ("all", "cast"):
            shape = (n,) + array.shape
        elif kind == "columns":
            shape = (n, array.shape[0], array.shape[1] // n)
        else:
            shape = array.shape
        dtype = jnp.bfloat16 if kind == "cast" else array.dtype
        shapes.append(jax.ShapeDtypeStruct(shape, dtype))
    count = len(items)
    return pl.pallas_call(
        functools.partial(exchange_kernel, n, kinds),
        out_shape=tuple(shapes),
        in_specs=[
            pl.BlockSpec(memory_space=pltpu.VMEM if kind == "cast" else pl.ANY) for kind in kinds
        ],
        out_specs=tuple([pl.BlockSpec(memory_space=pl.ANY)] * count),
        scratch_shapes=[
            pltpu.SemaphoreType.DMA((count, n)),
            pltpu.SemaphoreType.DMA((count, n)),
            pltpu.SemaphoreType.DMA((count,)),
        ]
        + [pltpu.VMEM(x.shape, jnp.bfloat16) for kind, x in items if kind == "cast"],
        compiler_params=pltpu.CompilerParams(collective_id=collective_id, has_side_effects=True),
        name=f"exchange_{collective_id}",
    )(*[array for _, array in items])


def fold(array):
    half = array.shape[-2] // 2
    return jnp.concatenate([array[..., :half, :], array[..., half:, :]], axis=-1)


def unfold(array):
    half = array.shape[-1] // 2
    return jnp.concatenate([array[..., :half], array[..., half:]], axis=-2)


def counts_item(counts, n):
    rows, columns = counts.shape
    width = columns // n
    if width % 128 == 0:
        return ("columns", counts)
    return ("parts", counts.reshape(rows, n, width).transpose(1, 0, 2))


def pack_links(link_gene, link_peak, link_weight, link_count):
    slots = link_gene.shape[0]
    live = jnp.where(jnp.arange(slots, dtype=jnp.int32) < link_count[0], link_weight, 0)
    gene, peak, live = [jnp.pad(x, (0, 128 - slots))[None, :] for x in (link_gene, link_peak, live)]
    row = lax.broadcasted_iota(jnp.int32, (8, 128), 0)
    return jnp.where(row == 0, gene, jnp.where(row == 1, peak, live))


def table_of(packed, slots, gene_blocks, peak_blocks):
    gene, peak, live = [packed[:, row, :slots].reshape(-1) for row in range(3)]
    gene_hot = (gene[None, :] == jnp.arange(gene_blocks, dtype=jnp.int32)[:, None]).astype(
        jnp.float32
    ) * live.astype(jnp.float32)[None, :]
    peak_hot = (peak[:, None] == jnp.arange(peak_blocks, dtype=jnp.int32)[None, :]).astype(
        jnp.float32
    )
    return jnp.dot(gene_hot, peak_hot, precision=HIGHEST)


def own_rows(table, columns, me):
    rows = max(columns // BLOCK, 1)
    return lax.dynamic_slice_in_dim(table, me * columns // BLOCK, rows, axis=0)


def couple(own_table, parts, columns, me):
    n, rank, width = parts.shape
    parts = parts.astype(jnp.float32)
    if width >= BLOCK:
        per = width // BLOCK
        table = own_table.reshape(own_table.shape[0], n, per)
        mixed = [
            sum(
                jnp.sum(
                    parts[:, :, j * BLOCK : (j + 1) * BLOCK] * table[r, :, j][:, None, None], axis=0
                )
                for j in range(per)
            )
            for r in range(own_table.shape[0])
        ]
    else:
        per = BLOCK // width
        split = parts.reshape(n // per, per, rank, width)
        mixed = []
        for r in range(own_table.shape[0]):
            pieces = jnp.sum(split * own_table[r][:, None, None, None], axis=0)
            mixed.append(jnp.concatenate([pieces[j] for j in range(per)], axis=1))
    mixed = mixed[0] if len(mixed) == 1 else jnp.concatenate(mixed, axis=1)
    if columns < BLOCK:
        mixed = lax.dynamic_slice_in_dim(mixed, lax.rem(me * columns, BLOCK), columns, axis=1)
    return mixed


def contract(left, right, axis_left, axis_right, **options):
    return lax.dot_general(
        left,
        right,
        (((axis_left,), (axis_right,)), ((), ())),
        preferred_element_type=jnp.float32,
        **options,
    )


def shards(
    rna_counts,
    atac_counts,
    cell_factor,
    gene_factor,
    peak_factor,
    link_gene,
    link_peak,
    link_weight,
    link_count,
):
    n = lax.axis_size("cells")
    me = lax.axis_index("cells")
    cells = rna_counts.shape[0]
    rank = cell_factor.shape[0]
    gene_width, peak_width = gene_factor.shape[1], peak_factor.shape[1]
    gene_blocks, peak_blocks = n * gene_width // BLOCK, n * peak_width // BLOCK
    link_scale = cells * n / 4.0

    cell_state = fold(cell_factor.T)
    packed, cell_parts, gene_parts, peak_parts, rna_all, atac_all = exchange(
        n,
        0,
        [
            ("all", pack_links(link_gene, link_peak, link_weight, link_count)),
            ("all", cell_state),
            ("cast", gene_factor),
            ("cast", peak_factor),
            counts_item(rna_counts, n),
            counts_item(atac_counts, n),
        ],
    )
    table = table_of(packed, link_gene.shape[0], gene_blocks, peak_blocks)
    to_genes = own_rows(table, gene_width, me)
    to_peaks = own_rows(table.T, peak_width, me)
    rna_all = rna_all.reshape(n * cells, gene_width)
    atac_all = atac_all.reshape(n * cells, peak_width)
    gene_state, peak_state = gene_factor, peak_factor
    for sweep_index in range(ROUNDS):
        cell_whole = unfold(cell_parts).reshape(n * cells, rank)
        gram_cells = contract(cell_whole, cell_whole, 0, 0, precision=HIGHEST)
        cell_low = cell_whole.astype(jnp.bfloat16)
        gene_num = contract(cell_low, rna_all, 0, 0) + link_scale * couple(
            to_genes, peak_parts, gene_width, me
        )
        peak_num = contract(cell_low, atac_all, 0, 0) + link_scale * couple(
            to_peaks, gene_parts, peak_width, me
        )
        gene_state = (
            gene_state * gene_num / (jnp.dot(gram_cells, gene_state, precision=HIGHEST) + EPSILON)
        )
        peak_state = (
            peak_state * peak_num / (jnp.dot(gram_cells, peak_state, precision=HIGHEST) + EPSILON)
        )
        gene_low = gene_state.astype(jnp.bfloat16)
        peak_low = peak_state.astype(jnp.bfloat16)
        gram_part = contract(gene_low, gene_low, 1, 1) + contract(peak_low, peak_low, 1, 1)
        cell_part = contract(rna_all, gene_low, 1, 1) + contract(atac_all, peak_low, 1, 1)
        gram_item = fold(gram_part)
        num_item = fold(cell_part.reshape(n, cells, rank))
        if sweep_index + 1 < ROUNDS:
            gene_parts, peak_parts, cell_parts, cell_state = between(
                n, 1 + sweep_index, gram_item, num_item, gene_low, peak_low, cell_state
            )
    cell_factor = unfold(cell_state).T
    gram_parts, num_parts = exchange(n, ROUNDS, [("all", gram_item), ("parts", num_item)])
    cell_num = unfold(jnp.sum(num_parts, axis=0)).T
    gram_features = unfold(jnp.sum(gram_parts, axis=0))
    cell_factor = (
        cell_factor * cell_num / (jnp.dot(gram_features, cell_factor, precision=HIGHEST) + EPSILON)
    )
    return (cell_factor, gene_state, peak_state)


def solution(mesh):
    rows = P(("groups", "cells"), None)
    columns = P(None, ("groups", "cells"))
    slots = P(("groups", "cells"))
    return jax.shard_map(
        shards,
        mesh=mesh,
        in_specs=(rows, rows, columns, columns, columns, slots, slots, slots, slots),
        out_specs=(columns, columns, columns),
        check_vma=False,
    )
```

```python
import functools
import math

import jax
import jax.numpy as jnp
from jax import lax
from jax.experimental import pallas as pl
from jax.experimental.pallas import tpu as pltpu
from jax.sharding import PartitionSpec as P

BLOCK = 128
CORES = 2
ROW = 4
ROUNDS = 2
EPSILON = 1e-06
HIGHEST = lax.Precision.HIGHEST
MESH = pl.DeviceIdType.MESH


class Routes:
    def __init__(self, n, kinds, ins, outs, send_sem, recv_sem, own_sem):
        self.n, self.kinds, self.ins, self.outs = n, kinds, ins, outs
        self.send_sem, self.recv_sem, self.own_sem = send_sem, recv_sem, own_sem
        self.me = lax.axis_index("cells")
        self.planes = n // (ROW * CORES)
        self.plane = self.me // (ROW * CORES)
        self.row = lax.rem(self.me // CORES, ROW)
        self.core = lax.rem(self.me, CORES)

    def greet(self):
        barrier = pltpu.get_barrier_semaphore()

        def signal(step, carry):
            peer = lax.rem(self.me + step, self.n)
            pl.semaphore_signal(
                barrier, inc=1, device_id={"cells": peer}, device_id_type=MESH
            )
            return carry

        lax.fori_loop(1, self.n, signal, 0)
        return lambda: pl.semaphore_wait(barrier, self.n - 1)

    def part(self, index, peer):
        kind = self.kinds[index]
        if kind == "all":
            return self.ins[index]
        if kind == "columns":
            width = self.outs[index].shape[2]
            return self.ins[index].at[:, pl.ds(pl.multiple_of(peer * width, 128), width)]
        return self.ins[index].at[peer]

    def own(self, index):
        return pltpu.make_async_copy(
            self.part(index, self.me), self.outs[index].at[self.me], self.own_sem.at[index]
        )

    def remote(self, index, step, peer, slot, source=None):
        return pltpu.make_async_remote_copy(
            src_ref=self.part(index, peer) if source is None else source,
            dst_ref=self.outs[index].at[slot],
            send_sem=self.send_sem.at[index, step],
            recv_sem=self.recv_sem.at[index, step],
            device_id={"cells": peer},
            device_id_type=MESH,
        )

    def place(self, plane_at, row_at, core_at):
        return (plane_at * ROW + row_at) * CORES + core_at

    def first(self, index, step):
        peer = self.place(lax.rem(self.plane + step, self.planes), self.row, self.core)
        return self.remote(index, step, peer, self.me)

    def second(self, index, step, turn, slot, source):
        peer = self.place(self.plane, (self.row + turn) % ROW, self.core)
        return self.remote(index, self.planes + step * (ROW - 1) + turn - 1, peer, slot, source)

    def third(self, index, step, turn, slot, source):
        peer = self.place(self.plane, self.row, 1 - self.core)
        return self.remote(index, self.planes * ROW + step * ROW + turn, peer, slot, source)

    def slot_of(self, step, turn, core_at):
        plane_at = lax.rem(self.plane + self.planes - step, self.planes)
        return self.place(plane_at, (self.row + ROW - turn) % ROW, core_at)

    def loop(self, low, high, body):
        def step_of(step, carry):
            body(step)
            return carry

        lax.fori_loop(low, high, step_of, 0)

    def start_all(self, items):
        def body(step):
            for index in items:
                self.first(index, step).start()

        self.loop(1, self.planes, body)
        for index in items:
            for turn in range(1, ROW):
                self.second(index, 0, turn, self.me, self.ins[index]).start()
            self.third(index, 0, 0, self.me, self.ins[index]).start()

    def relay_first(self, items):
        def body(step):
            slot = self.slot_of(step, 0, self.core)
            for index in items:
                block = self.outs[index].at[slot]
                self.remote(
                    index, step, self.place(self.plane, self.row, 1 - self.core), slot, block
                ).wait_recv()
                for turn in range(1, ROW):
                    self.second(index, step, turn, slot, block).start()
                self.third(index, step, 0, slot, block).start()

        self.loop(1, self.planes, body)

    def relay_second(self, items):
        def body(step):
            for turn in range(1, ROW):
                slot = self.slot_of(step, turn, self.core)
                for index in items:
                    block = self.outs[index].at[slot]
                    self.second(index, step, turn, slot, block).wait_recv()
                    self.third(index, step, turn, slot, block).start()

        self.loop(0, self.planes, body)

    def receive_third(self, items):
        def body(step):
            for turn in range(ROW):
                slot = self.slot_of(step, turn, 1 - self.core)
                for index in items:
                    self.third(index, step, turn, slot, self.outs[index].at[slot]).wait_recv()

        self.loop(0, self.planes, body)

    def end_all(self, items):
        def first(step):
            for index in items:
                self.first(index, step).wait_send()

        def later(step):
            for index in items:
                for turn in range(ROW):
                    if turn:
                        self.second(index, step, turn, self.me, self.ins[index]).wait_send()
                    self.third(index, step, turn, self.me, self.ins[index]).wait_send()

        self.loop(1, self.planes, first)
        self.loop(0, self.planes, later)

    def start_direct(self, items):
        steps = self.n - 1
        stride = next(k for k in range(self.n // 3, self.n) if math.gcd(k, steps) == 1)

        def body(turn):
            step = 1 + lax.rem(turn * stride, steps)
            for index in items:
                self.remote(index, step, lax.rem(self.me + step, self.n), self.me).start()

        self.loop(0, steps, body)

    def receive_direct(self, items):
        def body(step):
            source = lax.rem(self.me + self.n - step, self.n)
            peer = lax.rem(self.me + step, self.n)
            for index in items:
                self.remote(index, step, peer, source).wait_recv()

        self.loop(1, self.n, body)

    def end_direct(self, items):
        def body(step):
            for index in items:
                self.remote(index, step, lax.rem(self.me + step, self.n), self.me).wait_send()

        self.loop(1, self.n, body)


def exchange_kernel(n, kinds, *refs):
    count = len(kinds)
    ins, outs = list(refs[:count]), refs[count : 2 * count]
    casts = [index for index in range(count) if kinds[index] == "cast"]
    sems = refs[2 * count : 2 * count + 3]
    given = [ins[index] for index in casts]
    for index, low in zip(casts, refs[2 * count + 3 :]):
        ins[index] = low
    kinds = tuple("all" if kind == "cast" else kind for kind in kinds)
    routes = Routes(n, kinds, ins, outs, *sems)
    whole = [index for index in range(count) if kinds[index] == "all"]
    direct = [index for index in range(count) if kinds[index] != "all"]
    greeted = routes.greet()
    for index, wide in zip(casts, given):
        ins[index][...] = wide[...].astype(jnp.bfloat16)
    greeted()
    routes.start_all(whole)
    for index in range(count):
        routes.own(index).start()
    if direct:
        routes.start_direct(direct)
    routes.relay_first(whole)
    routes.relay_second(whole)
    routes.receive_third(whole)
    if direct:
        routes.receive_direct(direct)
        routes.end_direct(direct)
    routes.end_all(whole)
    for index in range(count):
        routes.own(index).wait()


def between_kernel(
    n, gram, num, gene, peak, cell, gene_parts, peak_parts, cell_parts, cell_new,
    gram_parts, num_parts, *sems
):
    routes = Routes(
        n,
        ("all", "parts", "all", "all", "all"),
        (gram, num, gene, peak, cell_new),
        (gram_parts, num_parts, gene_parts, peak_parts, cell_parts),
        *sems,
    )
    greeted = routes.greet()
    for index in range(4):
        routes.own(index).start()
    greeted()
    routes.start_all([0])
    routes.start_direct([1])
    routes.start_all([2, 3])
    routes.relay_first([0])
    routes.relay_second([0])
    routes.relay_first([2, 3])
    routes.receive_third([0])
    routes.receive_direct([1])
    routes.own(0).wait()
    routes.own(1).wait()
    folded = jnp.sum(gram_parts[...], axis=0)
    rank = folded.shape[1] // 2
    turned = pltpu.roll(folded, rank, 1)
    left = lax.broadcasted_iota(jnp.int32, folded.shape, 1) < rank
    square = jnp.concatenate(
        [
            jnp.where(left, folded, 0.0),
            jnp.where(left, turned, 0.0),
            jnp.where(left, 0.0, turned),
            jnp.where(left, 0.0, folded),
        ],
        axis=0,
    )
    denominator = jnp.dot(
        cell[...], square, precision=HIGHEST, preferred_element_type=jnp.float32
    )
    cell_new[...] = cell[...] * jnp.sum(num_parts[...], axis=0) / (denominator + EPSILON)
    routes.own(4).start()
    routes.start_all([4])
    routes.relay_second([2, 3])
    routes.relay_first([4])
    routes.relay_second([4])
    routes.receive_third([2, 3, 4])
    routes.end_direct([1])
    routes.end_all([0, 2, 3, 4])
    for index in range(2, 5):
        routes.own(index).wait()


def between(n, collective_id, gram, num, gene, peak, cell):
    anywhere = pl.BlockSpec(memory_space=pl.ANY)
    vmem = pl.BlockSpec(memory_space=pltpu.VMEM)
    gathered = [jax.ShapeDtypeStruct((n,) + x.shape, x.dtype) for x in (gene, peak, cell)]
    return pl.pallas_call(
        functools.partial(between_kernel, n),
        out_shape=(*gathered, jax.ShapeDtypeStruct(cell.shape, cell.dtype)),
        in_specs=[anywhere] * 4 + [vmem],
        out_specs=(anywhere, anywhere, anywhere, vmem),
        scratch_shapes=[
            pltpu.VMEM((n,) + gram.shape, gram.dtype),
            pltpu.VMEM(num.shape, num.dtype),
            pltpu.SemaphoreType.DMA((5, n)),
            pltpu.SemaphoreType.DMA((5, n)),
            pltpu.SemaphoreType.DMA((5,)),
        ],
        compiler_params=pltpu.CompilerParams(collective_id=collective_id, has_side_effects=True),
        name=f"between_{collective_id}",
    )(gram, num, gene, peak, cell)


def exchange(n, collective_id, items):
    kinds = tuple(kind for kind, _ in items)
    shapes = []
    for kind, array in items:
        if kind in ("all", "cast"):
            shape = (n,) + array.shape
        elif kind == "columns":
            shape = (n, array.shape[0], array.shape[1] // n)
        else:
            shape = array.shape
        dtype = jnp.bfloat16 if kind == "cast" else array.dtype
        shapes.append(jax.ShapeDtypeStruct(shape, dtype))
    count = len(items)
    return pl.pallas_call(
        functools.partial(exchange_kernel, n, kinds),
        out_shape=tuple(shapes),
        in_specs=[
            pl.BlockSpec(memory_space=pltpu.VMEM if kind == "cast" else pl.ANY) for kind in kinds
        ],
        out_specs=tuple([pl.BlockSpec(memory_space=pl.ANY)] * count),
        scratch_shapes=[
            pltpu.SemaphoreType.DMA((count, n)),
            pltpu.SemaphoreType.DMA((count, n)),
            pltpu.SemaphoreType.DMA((count,)),
        ]
        + [pltpu.VMEM(x.shape, jnp.bfloat16) for kind, x in items if kind == "cast"],
        compiler_params=pltpu.CompilerParams(collective_id=collective_id, has_side_effects=True),
        name=f"exchange_{collective_id}",
    )(*[array for _, array in items])


def fold(array):
    half = array.shape[-2] // 2
    return jnp.concatenate([array[..., :half, :], array[..., half:, :]], axis=-1)


def unfold(array):
    half = array.shape[-1] // 2
    return jnp.concatenate([array[..., :half], array[..., half:]], axis=-2)


def counts_item(counts, n):
    rows, columns = counts.shape
    width = columns // n
    if width % 128 == 0:
        return ("columns", counts)
    return ("parts", counts.reshape(rows, n, width).transpose(1, 0, 2))


def pack_links(link_gene, link_peak, link_weight, link_count):
    slots = link_gene.shape[0]
    live = jnp.where(jnp.arange(slots, dtype=jnp.int32) < link_count[0], link_weight, 0)
    gene, peak, live = [jnp.pad(x, (0, 128 - slots))[None, :] for x in (link_gene, link_peak, live)]
    row = lax.broadcasted_iota(jnp.int32, (8, 128), 0)
    return jnp.where(row == 0, gene, jnp.where(row == 1, peak, live))


def table_of(packed, slots, gene_blocks, peak_blocks):
    gene, peak, live = [packed[:, row, :slots].reshape(-1) for row in range(3)]
    gene_hot = (gene[None, :] == jnp.arange(gene_blocks, dtype=jnp.int32)[:, None]).astype(
        jnp.float32
    ) * live.astype(jnp.float32)[None, :]
    peak_hot = (peak[:, None] == jnp.arange(peak_blocks, dtype=jnp.int32)[None, :]).astype(
        jnp.float32
    )
    return jnp.dot(gene_hot, peak_hot, precision=HIGHEST)


def own_rows(table, columns, me):
    rows = max(columns // BLOCK, 1)
    return lax.dynamic_slice_in_dim(table, me * columns // BLOCK, rows, axis=0)


def couple(own_table, parts, columns, me):
    n, rank, width = parts.shape
    parts = parts.astype(jnp.float32)
    if width >= BLOCK:
        per = width // BLOCK
        table = own_table.reshape(own_table.shape[0], n, per)
        mixed = [
            sum(
                jnp.sum(
                    parts[:, :, j * BLOCK : (j + 1) * BLOCK] * table[r, :, j][:, None, None], axis=0
                )
                for j in range(per)
            )
            for r in range(own_table.shape[0])
        ]
    else:
        per = BLOCK // width
        split = parts.reshape(n // per, per, rank, width)
        mixed = []
        for r in range(own_table.shape[0]):
            pieces = jnp.sum(split * own_table[r][:, None, None, None], axis=0)
            mixed.append(jnp.concatenate([pieces[j] for j in range(per)], axis=1))
    mixed = mixed[0] if len(mixed) == 1 else jnp.concatenate(mixed, axis=1)
    if columns < BLOCK:
        mixed = lax.dynamic_slice_in_dim(mixed, lax.rem(me * columns, BLOCK), columns, axis=1)
    return mixed


def contract(left, right, axis_left, axis_right, **options):
    return lax.dot_general(
        left,
        right,
        (((axis_left,), (axis_right,)), ((), ())),
        preferred_element_type=jnp.float32,
        **options,
    )


def shards(
    rna_counts,
    atac_counts,
    cell_factor,
    gene_factor,
    peak_factor,
    link_gene,
    link_peak,
    link_weight,
    link_count,
):
    n = lax.axis_size("cells")
    me = lax.axis_index("cells")
    cells = rna_counts.shape[0]
    rank = cell_factor.shape[0]
    gene_width, peak_width = gene_factor.shape[1], peak_factor.shape[1]
    gene_blocks, peak_blocks = n * gene_width // BLOCK, n * peak_width // BLOCK
    link_scale = cells * n / 4.0

    cell_state = fold(cell_factor.T)
    packed, cell_parts, gene_parts, peak_parts, rna_all, atac_all = exchange(
        n,
        0,
        [
            ("all", pack_links(link_gene, link_peak, link_weight, link_count)),
            ("all", cell_state),
            ("cast", gene_factor),
            ("cast", peak_factor),
            counts_item(rna_counts, n),
            counts_item(atac_counts, n),
        ],
    )
    table = table_of(packed, link_gene.shape[0], gene_blocks, peak_blocks)
    to_genes = own_rows(table, gene_width, me)
    to_peaks = own_rows(table.T, peak_width, me)
    rna_all = rna_all.reshape(n * cells, gene_width)
    atac_all = atac_all.reshape(n * cells, peak_width)
    gene_state, peak_state = gene_factor, peak_factor
    for sweep_index in range(ROUNDS):
        cell_whole = unfold(cell_parts).reshape(n * cells, rank)
        gram_cells = contract(cell_whole, cell_whole, 0, 0, precision=HIGHEST)
        cell_low = cell_whole.astype(jnp.bfloat16)
        gene_num = contract(cell_low, rna_all, 0, 0) + link_scale * couple(
            to_genes, peak_parts, gene_width, me
        )
        peak_num = contract(cell_low, atac_all, 0, 0) + link_scale * couple(
            to_peaks, gene_parts, peak_width, me
        )
        gene_state = (
            gene_state * gene_num / (jnp.dot(gram_cells, gene_state, precision=HIGHEST) + EPSILON)
        )
        peak_state = (
            peak_state * peak_num / (jnp.dot(gram_cells, peak_state, precision=HIGHEST) + EPSILON)
        )
        gene_low = gene_state.astype(jnp.bfloat16)
        peak_low = peak_state.astype(jnp.bfloat16)
        gram_part = contract(gene_low, gene_low, 1, 1) + contract(peak_low, peak_low, 1, 1)
        cell_part = contract(rna_all, gene_low, 1, 1) + contract(atac_all, peak_low, 1, 1)
        gram_item = fold(gram_part)
        num_item = fold(cell_part.reshape(n, cells, rank))
        if sweep_index + 1 < ROUNDS:
            gene_parts, peak_parts, cell_parts, cell_state = between(
                n, 1 + sweep_index, gram_item, num_item, gene_low, peak_low, cell_state
            )
    cell_factor = unfold(cell_state).T
    gram_parts, num_parts = exchange(n, ROUNDS, [("all", gram_item), ("parts", num_item)])
    cell_num = unfold(jnp.sum(num_parts, axis=0)).T
    gram_features = unfold(jnp.sum(gram_parts, axis=0))
    cell_factor = (
        cell_factor * cell_num / (jnp.dot(gram_features, cell_factor, precision=HIGHEST) + EPSILON)
    )
    return (cell_factor, gene_state, peak_state)


def solution(mesh):
    rows = P(("groups", "cells"), None)
    columns = P(None, ("groups", "cells"))
    slots = P(("groups", "cells"))
    return jax.shard_map(
        shards,
        mesh=mesh,
        in_specs=(rows, rows, columns, columns, columns, slots, slots, slots, slots),
        out_specs=(columns, columns, columns),
        check_vma=False,
    )
```
